32 devices in a mesh: shard: 2 (over y), ctx: 4 (over x, core), tp: 4 (over z).
Axes of the slice: x: 2, y: 2, z: 4, core: 2. Of those that a mesh axis runs over, the one named last changes fastest.
Arguments:
- video: bfloat16 [2, 16, 16, 16, 1152], P('shard', 'ctx', 'tp'), may hold values from -6 to 6
- cond: bfloat16 [2, 1152], P('shard'), may hold values from -6 to 6
- w_ada: bfloat16 [2, 1152, 6912], P(None, 'shard', 'tp'), may hold values from -0.1875 to 0.1875
- b_ada: bfloat16 [2, 6912], P(None, 'tp'), may hold values from 0.5 to 1.5
- w_qkv: bfloat16 [2, 3, 1152, 1152], P(None, None, 'shard', 'tp'), may hold values from -0.09375 to 0.09375
- b_qv: bfloat16 [2, 2, 1152], P(None, None, 'tp'), may hold values from -3 to 3
- w_out: bfloat16 [2, 1152, 1152], P(None, 'tp', 'shard'), may hold values from -0.75 to 0.75
- b_out: bfloat16 [2, 1152], replicated, may hold values from -3 to 3
- w_up: bfloat16 [2, 1152, 4608], P(None, 'shard', 'tp'), may hold values from -0.09375 to 0.09375
- b_up: bfloat16 [2, 4608], P(None, 'tp'), may hold values from -3 to 3
- w_down: bfloat16 [2, 4608, 1152], P(None, 'tp', 'shard'), may hold values from -0.09375 to 0.09375
- b_down: bfloat16 [2, 1152], replicated, may hold values from -3 to 3
- cotangent: bfloat16 [2, 16, 16, 16, 1152], P('shard', None, 'tp', 'ctx'), may hold values from -6 to 6
Outputs:
- out: bfloat16 [2, 16, 16, 16, 1152], P('shard', None, 'tp', 'ctx')
- grad_video: float32 [2, 16, 16, 16, 1152], P('shard', 'ctx', 'tp')
- grad_cond: float32 [2, 1152], P('shard')
- grad_w_ada: float32 [2, 1152, 6912], P(None, 'shard', 'tp')
- grad_b_ada: float32 [2, 6912], P(None, 'tp')
- grad_w_qkv: float32 [2, 3, 1152, 1152], P(None, None, 'shard', 'tp')
- grad_b_qv: float32 [2, 2, 1152], P(None, None, 'tp')
- grad_w_out: float32 [2, 1152, 1152], P(None, 'tp', 'shard')
- grad_b_out: float32 [2, 1152], replicated
- grad_w_up: float32 [2, 1152, 4608], P(None, 'shard', 'tp')
- grad_b_up: float32 [2, 4608], P(None, 'tp')
- grad_w_down: float32 [2, 4608, 1152], P(None, 'tp', 'shard')
- grad_b_down: float32 [2, 1152], replicated
The draws below stay inside these ranges and needn't reach their ends.
All inputs are finite; a program needn't handle non-finite values.
Results may differ from the reference program's by a relative error of at most 0.025.
Values may be sent and summed in bfloat16 or wider, within the bound.
No kernel may reach another device: no remote copies, remote signals or barrier semaphores. Data moves between devices by JAX's collectives and lax.ppermute only.
A program may use at most 256 MiB of HBM per device.

```python
import math
import jax
import jax.numpy as jnp
from jax import lax

D = 1152
HEADS = 16
HEAD_DIM = 72
FF = 4608
FRAMES = 16
HP = 16
WP = 16
CLIPS = 2


def strengthened(values, stream_key, source, target, parts, factor):
    owner, partner = [(jnp.arange(values.shape[dim]) // (values.shape[dim] // parts)).reshape([-1 if axis == dim else 1 for axis in range(values.ndim)]) for dim in (source, target)]
    chosen = jax.random.permutation(stream_key, parts)[partner]
    strong = (owner == chosen) | (owner == (partner + parts // 2) % parts)
    return jnp.where(strong, factor * values, values)


def steps_of(own_key, shape, cuts, least, high):
    factor_of, own = 1.0, jax.random.fold_in(own_key, 6)
    for position, blocks in cuts:
        steps = jnp.exp(jax.random.uniform(jax.random.fold_in(own, position), (blocks,), jnp.float32, least / len(cuts), high / len(cuts)))
        factor_of = factor_of * jnp.repeat(steps, shape[position] // blocks).reshape([-1 if axis == position else 1 for axis in range(len(shape))])
    return factor_of


def normal_values(rng, shape, scale, reach, cuts=(), kind=jnp.bfloat16):
    level = steps_of(rng, shape, cuts, -0.22, 0.18) if cuts else 1.0
    values = jax.random.normal(rng, shape, jnp.float32) * scale * level
    return jnp.minimum(jnp.maximum(values, -reach), reach).astype(kind)


def gaussian_with(own_key, extent, scale, limit, shards, heavy, held_as=jnp.bfloat16):
    drawn = scale * jax.random.normal(own_key, extent, jnp.float32)
    if shards:
        drawn = drawn * steps_of(own_key, extent, shards, -0.22, 0.18)
    return jnp.clip(strengthened(drawn, jax.random.fold_in(own_key, 3), *heavy), -limit, limit).astype(held_as)


def setup_inputs(seed: int = 0) -> dict:
    streams_of = jax.random.split(jax.random.key(seed), 14)
    video = normal_values(streams_of[0], (CLIPS, FRAMES, HP, WP, D), 1.0, 6.0, ((0, 2), (1, 4), (2, 4)))
    cond = normal_values(streams_of[1], (CLIPS, D), 1.0, 6.0, ((0, 2),))
    w_ada = normal_values(streams_of[2], (2, D, 6 * D), D ** -0.5, 0.1875, ((1, 2), (2, 4)))
    b_ada = jnp.clip(1.0 + 0.1 * jax.random.normal(streams_of[3], (2, 6 * D), jnp.float32), 0.5, 1.5).astype(jnp.bfloat16)
    w_qkv = normal_values(streams_of[4], (2, 3, D, D), (4 * D) ** -0.5, 0.09375, ((2, 2), (3, 4)))
    b_qv = normal_values(streams_of[5], (2, 2, D), 0.5, 3.0, ((2, 4),))
    w_out = normal_values(streams_of[6], (2, D, D), (D // 16) ** -0.5, 0.75, ((1, 4), (2, 2)))
    b_out = normal_values(streams_of[7], (2, D), 0.5, 3.0)
    w_up = normal_values(streams_of[8], (2, D, FF), (4 * D) ** -0.5, 0.09375, ((1, 2), (2, 4)))
    b_up = normal_values(streams_of[9], (2, FF), 0.5, 3.0, ((1, 4),))
    w_down = normal_values(streams_of[10], (2, FF, D), FF ** -0.5, 0.09375, ((1, 4), (2, 2)))
    b_down = normal_values(streams_of[11], (2, D), 0.5, 3.0)
    cotangent = gaussian_with(streams_of[12], (CLIPS, FRAMES, HP, WP, D), 1.0, 6.0, ((0, 2), (2, 4), (3, 4)), (0, 4, 2, 2.0))
    return {"video": video, "cond": cond, "w_ada": w_ada, "b_ada": b_ada, "w_qkv": w_qkv, "b_qv": b_qv, "w_out": w_out, "b_out": b_out, "w_up": w_up, "b_up": b_up, "w_down": w_down, "b_down": b_down, "cotangent": cotangent}


@jax.custom_vjp
def low(v):
    return lax.optimization_barrier(v.astype(jnp.bfloat16)).astype(jnp.float32)

@jax.custom_vjp
def low_back(v):
    return v

def low_keep(v):
    return (low(v), None)

def low_pass(kept, grad):
    return (grad,)

def back_keep(v):
    return (v, None)

def back_low(kept, grad):
    return (low(grad),)
low.defvjp(low_keep, low_pass)
low_back.defvjp(back_keep, back_low)
highest = lax.Precision.HIGHEST

def rounded(value):
    return low_back(low(value))

def matmul(left, right):
    return jnp.dot(left, right, precision=highest, preferred_element_type=jnp.float32)

def layer_norm(values):
    average = lax.optimization_barrier(jnp.mean(values, axis=-1, keepdims=True))
    centered = values - average
    spread = lax.optimization_barrier(jnp.mean(centered * centered, axis=-1, keepdims=True))
    return centered * lax.rsqrt(spread + 1e-06)

def attend_group(query_seq, key_seq, value_seq):
    factor = 1.0 / math.sqrt(HEAD_DIM)
    scores = low_back(jnp.einsum('gqhe,gkhe->ghqk', query_seq, key_seq, precision=highest) * factor)
    weights = low(jax.nn.softmax(scores, axis=-1))
    return jnp.einsum('ghqk,gkhe->gqhe', weights, value_seq, precision=highest)

def attention(query_seq, key_seq, value_seq):
    batch = query_seq.shape[0]
    length = query_seq.shape[1]
    group = math.gcd(batch, max(1, 4096 // length))
    shape = (batch // group, group) + query_seq.shape[1:]
    blocked = jax.checkpoint(attend_group)
    result = lax.map(lambda triple: blocked(triple[0], triple[1], triple[2]), (query_seq.reshape(shape), key_seq.reshape(shape), value_seq.reshape(shape)))
    return result.reshape(query_seq.shape)

def to_sequences(rows, grid, temporal):
    heads = rows.reshape(grid + (HEADS, HEAD_DIM))
    if temporal:
        heads = jnp.transpose(heads, (0, 2, 3, 1, 4, 5))
        return heads.reshape(grid[0] * grid[2] * grid[3], grid[1], HEADS, HEAD_DIM)
    return heads.reshape(grid[0] * grid[1], grid[2] * grid[3], HEADS, HEAD_DIM)

def from_sequences(heads, grid, temporal):
    if temporal:
        heads = heads.reshape(grid[0], grid[2], grid[3], grid[1], HEADS, HEAD_DIM)
        heads = jnp.transpose(heads, (0, 3, 1, 2, 4, 5))
    return heads.reshape(-1, HEADS * HEAD_DIM)

def block(inputs, cond_act, w_ada, b_ada, w_qkv, b_qv, w_out, b_out, w_up, b_up, w_down, b_down, temporal):
    grid = inputs.shape[:4]
    modulation = matmul(cond_act, w_ada) + b_ada
    pieces = modulation.reshape(grid[0], 6, 1, 1, 1, D)
    shift_a, scale_a, gate_a, shift_m, scale_m, gate_m = [pieces[:, number] for number in range(6)]
    hidden = low(layer_norm(inputs) * (1.0 + scale_a) + shift_a).reshape(-1, D)
    query_rows = rounded(matmul(hidden, w_qkv[0]) + b_qv[0])
    key_rows = rounded(matmul(hidden, w_qkv[1]))
    value_rows = rounded(matmul(hidden, w_qkv[2]) + b_qv[1])
    attended = attention(to_sequences(query_rows, grid, temporal), to_sequences(key_rows, grid, temporal), to_sequences(value_rows, grid, temporal))
    attended = rounded(from_sequences(attended, grid, temporal))
    attn_out = low_back(matmul(attended, w_out) + b_out).reshape(inputs.shape)
    after_attn = inputs + gate_a * attn_out
    hidden_two = low(layer_norm(after_attn) * (1.0 + scale_m) + shift_m).reshape(-1, D)
    up_rows = low_back(matmul(hidden_two, w_up) + b_up)
    activated = low(jax.nn.gelu(up_rows, approximate=True))
    mlp_out = low_back(matmul(activated, w_down) + b_down).reshape(inputs.shape)
    return after_attn + gate_m * mlp_out

def reference(video, cond, w_ada, b_ada, w_qkv, b_qv, w_out, b_out, w_up, b_up, w_down, b_down, cotangent):
    params = tuple((array.astype(jnp.float32) for array in (w_ada, b_ada, w_qkv, b_qv, w_out, b_out, w_up, b_up, w_down, b_down)))

    def forward(video_f, cond_f, weights):
        cond_act = low(jax.nn.silu(cond_f))
        first = [weight[0] for weight in weights]
        second = [weight[1] for weight in weights]
        middle = rounded(block(video_f, cond_act, first[0], first[1], first[2], first[3], first[4], first[5], first[6], first[7], first[8], first[9], False))
        return block(middle, cond_act, second[0], second[1], second[2], second[3], second[4], second[5], second[6], second[7], second[8], second[9], True)
    result, pullback = jax.vjp(forward, video.astype(jnp.float32), cond.astype(jnp.float32), params)
    grad_video, grad_cond, grads = pullback(cotangent.astype(jnp.float32))
    return (result.astype(jnp.bfloat16), grad_video, grad_cond, grads[0], grads[1], grads[2], grads[3], grads[4], grads[5], grads[6], grads[7], grads[8], grads[9])
```

```python
from functools import partial
import math

import jax
import jax.numpy as jnp
from jax import lax
from jax.experimental import pallas as pl
from jax.experimental.pallas import tpu as pltpu
from jax.sharding import PartitionSpec as P

HEAD_DIM = 72
GROUP = 256

bf16 = jnp.bfloat16
f32 = jnp.float32
highest = lax.Precision.HIGHEST


def layer_norm(values):
    average = jnp.mean(values, axis=-1, keepdims=True)
    centered = values - average
    spread = jnp.mean(centered * centered, axis=-1, keepdims=True)
    return centered * lax.rsqrt(spread + 1e-06)


def modulate(values, offset, factor):
    return layer_norm(values) * (1.0 + factor) + offset


def dot_nt(left, right):
    return lax.dot_general(left, right, (((1,), (1,)), ((), ())), preferred_element_type=f32)


def dot_nn(left, right):
    return lax.dot_general(left, right, (((1,), (0,)), ((), ())), preferred_element_type=f32)


def dot_tn(left, right):
    return lax.dot_general(left, right, (((0,), (0,)), ((), ())), preferred_element_type=f32)


def swap(values, axis, bit):
    count = lax.axis_size(axis)
    return lax.ppermute(values, axis, [(i, i ^ bit) for i in range(count)])


def bits_of(axis):
    count = lax.axis_size(axis)
    assert count & (count - 1) == 0
    found = []
    while count > 1:
        count //= 2
        found.append(count)
    return found


def spread(values, axis="ctx"):
    slots = {0: values}
    for bit in bits_of(axis):
        for key in list(slots):
            slots[key ^ bit] = swap(slots[key], axis, bit)
    return [slots[key] for key in range(len(slots))]


def collect(terms, axis="ctx"):
    slots = dict(enumerate(terms))
    for bit in reversed(bits_of(axis)):
        for key in sorted((k for k in slots if k & bit), reverse=True):
            sent = swap(slots.pop(key).astype(bf16), axis, bit)
            slots[key ^ bit] = slots[key ^ bit] + sent.astype(f32)
    return slots[0]


def sum_over(values, axis):
    for bit in reversed(bits_of(axis)):
        values = values + swap(values, axis, bit)
    return values


def shifted(values, axis, shift):
    count = lax.axis_size(axis)
    return lax.ppermute(values, axis, [(i, (i + shift) % count) for i in range(count)])


def small_gather(values, axis):
    count = lax.axis_size(axis)
    own = lax.axis_index(axis)
    parts = jnp.stack([values] + [shifted(values, axis, k) for k in range(1, count)])
    return jnp.take(parts, (own - jnp.arange(count)) % count, axis=0)


def small_exchange(values, axis):
    count = lax.axis_size(axis)
    own = lax.axis_index(axis)
    pick = lambda k: lax.dynamic_index_in_dim(values, (own + k) % count, 0, keepdims=False)
    return [pick(0)] + [shifted(pick(k), axis, k) for k in range(1, count)]


def small_scatter(values, axis):
    return sum(small_exchange(values, axis))


def small_all_to_all(values, axis):
    count = lax.axis_size(axis)
    own = lax.axis_index(axis)
    parts = jnp.stack(small_exchange(values, axis))
    return jnp.take(parts, (own - jnp.arange(count)) % count, axis=0)


def turn(values):
    count = lax.axis_size("ctx")
    assert count == lax.axis_size("tp")
    pairs = [(i * count + j, j * count + i) for i in range(count) for j in range(count)]
    return lax.ppermute(values, ("ctx", "tp"), pairs)


def group_mask(seen):
    row = lax.broadcasted_iota(jnp.int32, (GROUP, GROUP), 0)
    column = lax.broadcasted_iota(jnp.int32, (GROUP, GROUP), 1)
    return (row % seen) == (column % seen)


def probs_of(query, key, own_head, seen):
    scores = dot_nt(query * own_head, key) * (1.0 / math.sqrt(HEAD_DIM))
    if seen > 1:
        scores = jnp.where(group_mask(seen), scores, -1e30)
    weights = jnp.exp(scores - jnp.max(scores, axis=-1, keepdims=True))
    return weights * (1.0 / jnp.sum(weights, axis=-1, keepdims=True))


def attend_kernel(heads_ref, qkv_ref, out_ref, *, seen):
    cut = lambda n: qkv_ref[n].reshape(GROUP, qkv_ref.shape[-1])
    query, key, value = cut(0), cut(1), cut(2)
    total = None
    for head in range(heads_ref.shape[0]):
        own_head = heads_ref[head : head + 1, :]
        probs = probs_of(query, key, own_head, seen)
        part = dot_nn(probs.astype(bf16), value * own_head)
        total = part if total is None else total + part
    out_ref[...] = total.astype(bf16).reshape(out_ref.shape)


def attend_back_kernel(heads_ref, qkv_ref, grad_ref, out_ref, *, seen):
    cut = lambda n: qkv_ref[n].reshape(GROUP, qkv_ref.shape[-1])
    query, key, value = cut(0), cut(1), cut(2)
    grad = grad_ref[...].reshape(GROUP, grad_ref.shape[-1])
    factor = 1.0 / math.sqrt(HEAD_DIM)
    totals = [None, None, None]
    for head in range(heads_ref.shape[0]):
        own_head = heads_ref[head : head + 1, :]
        probs = probs_of(query, key, own_head, seen)
        own_grad = grad * own_head
        grad_value = dot_tn(probs.astype(bf16), own_grad)
        grad_probs = dot_nt(own_grad, value)
        inner = jnp.sum(grad_probs * probs, axis=-1, keepdims=True)
        grad_scores = (probs * (grad_probs - inner)).astype(bf16)
        grad_query = dot_nn(grad_scores, key * own_head)
        grad_key = dot_tn(grad_scores, query * own_head)
        parts = (grad_query, grad_key, grad_value)
        totals = [p if t is None else t + p for t, p in zip(totals, parts)]
    for number, scale in enumerate((factor, factor, 1.0)):
        result = (totals[number] * scale).astype(bf16)
        out_ref[number] = result.reshape(out_ref.shape[1:])


def head_masks(columns):
    head = jnp.arange(columns)[None, :] // HEAD_DIM
    return (head == jnp.arange(columns // HEAD_DIM)[:, None]).astype(bf16)


def group_specs(rows, columns, parts):
    slot = GROUP // parts
    groups = rows // GROUP
    shape = (parts, groups, slot, columns)
    block = (parts, 1, slot, columns)
    plain = pl.BlockSpec(block, lambda g: (0, g, 0, 0))
    stacked = pl.BlockSpec((3,) + block, lambda g: (0, 0, g, 0, 0))
    heads = pl.BlockSpec((columns // HEAD_DIM, columns), lambda g: (0, 0))
    return groups, shape, heads, plain, stacked


def attend(qkv, parts, seen):
    rows, columns = qkv.shape[1:]
    groups, shape, heads, plain, stacked = group_specs(rows, columns, parts)
    result = pl.pallas_call(
        partial(attend_kernel, seen=seen),
        grid=(groups,),
        in_specs=[heads, stacked],
        out_specs=plain,
        out_shape=jax.ShapeDtypeStruct(shape, bf16),
        name="attend",
    )(head_masks(columns), qkv.reshape((3,) + shape))
    return result.reshape(rows, columns)


def attend_back(qkv, grad, parts, seen):
    rows, columns = qkv.shape[1:]
    groups, shape, heads, plain, stacked = group_specs(rows, columns, parts)
    result = pl.pallas_call(
        partial(attend_back_kernel, seen=seen),
        grid=(groups,),
        in_specs=[heads, stacked, plain],
        out_specs=stacked,
        out_shape=jax.ShapeDtypeStruct((3,) + shape, bf16),
        name="attend_back",
    )(head_masks(columns), qkv.reshape((3,) + shape), grad.reshape(shape))
    return result.reshape(3, rows, columns)


def own_part(values, axis):
    count = lax.axis_size("ctx")
    split = values.shape[axis] // count
    return lax.dynamic_slice_in_dim(values, lax.axis_index("ctx") * split, split, axis)


def fetch(piece):
    shards, quarters = lax.axis_size("shard"), lax.axis_size("tp")
    units, columns = piece.shape
    whole = lax.all_gather(piece[None], ("shard", "tp"), axis=0, tiled=True)
    whole = whole.reshape(shards, quarters, units, columns)
    return jnp.transpose(whole, (1, 2, 0, 3))


def fetch_block(number, w_qkv, w_out, w_up, w_down):
    quarters = lax.axis_size("tp")
    width = w_out.shape[2] * lax.axis_size("shard")
    qkv = jnp.transpose(own_part(w_qkv[number], 2), (0, 2, 1))
    units = qkv.shape[1]
    attn = jnp.concatenate([qkv.reshape(3 * units, -1), own_part(w_out[number], 0)])
    attn = fetch(attn).reshape(quarters, 4, units, width)
    attn = jnp.transpose(attn, (1, 0, 2, 3)).reshape(4, quarters * units, width)
    up = fetch(jnp.transpose(own_part(w_up[number], 1))).reshape(-1, width)
    down = fetch(own_part(w_down[number], 0)).reshape(-1, width)
    return (attn[:3], attn[3], up, down)


def reduce_weights(grad):
    shards = lax.axis_size("shard")
    quarters, units, width = grad.shape
    pieces = grad.astype(bf16).reshape(quarters, units, shards, width // shards)
    pieces = jnp.transpose(pieces, (2, 0, 1, 3)).reshape(shards * quarters, units, -1)
    own = lax.psum_scatter(pieces, ("shard", "tp"), scatter_dimension=0, tiled=True)
    own = own.reshape(units, width // shards)
    slots = spread(own)
    order = jnp.arange(len(slots)) ^ lax.axis_index("ctx")
    return jnp.take(jnp.stack(slots), order, axis=0).astype(f32)


def forward_block(inputs, modulation, weights, b_qv, b_out, b_up, b_down, parts, seen):
    w_qkv, w_out, w_up, w_down = weights
    own_rows = inputs.shape[0]
    shift_a, scale_a, gate_a, shift_m, scale_m, gate_m = modulation
    hidden = jnp.concatenate(spread(modulate(inputs, shift_a, scale_a).astype(bf16)))
    projected = jnp.einsum("rd,tcd->trc", hidden, w_qkv, preferred_element_type=f32)
    bias = jnp.stack([b_qv[0], jnp.zeros_like(b_qv[0]), b_qv[1]])
    qkv = (projected + bias[:, None, :]).astype(bf16)
    attended = attend(qkv, parts, seen)
    attn_out = reduce_product(attended, w_out, own_rows) + b_out
    after_attn = inputs + gate_a * attn_out
    hidden_two = jnp.concatenate(spread(modulate(after_attn, shift_m, scale_m).astype(bf16)))
    up_rows = dot_nt(hidden_two, w_up) + b_up
    activated = jax.nn.gelu(up_rows, approximate=True).astype(bf16)
    mlp_out = reduce_product(activated, w_down, own_rows) + b_down
    result = after_attn + gate_m * mlp_out
    kept = (inputs, after_attn, hidden, qkv, attended, attn_out, hidden_two, up_rows, mlp_out)
    return (result, kept)


def reduce_product(left, right, own_rows):
    count = left.shape[0] // own_rows
    half = (count // 2) * own_rows
    far = dot_nn(left[half:], right)
    near = dot_nn(left[:half], right)
    cut = lambda rows: [rows[n : n + own_rows] for n in range(0, half, own_rows)]
    return collect(cut(near) + cut(far))


def backward_block(grad_y, kept, modulation, weights, parts, seen):
    inputs, after_attn, hidden, qkv, attended, attn_out, hidden_two, up_rows, mlp_out = kept
    w_qkv, w_out, w_up, w_down = weights
    own_rows = inputs.shape[0]
    quarters = lax.axis_size("tp")
    shift_a, scale_a, gate_a, shift_m, scale_m, gate_m = modulation
    token_sum = lambda values: jnp.sum(values, axis=0, keepdims=True, dtype=f32)

    grad_mlp = (gate_m * grad_y).astype(bf16)
    grad_rows = jnp.concatenate(spread(grad_mlp))
    grad_gate_m = token_sum(grad_y * mlp_out)
    grad_b_down = token_sum(grad_mlp)
    activated, gelu_back = jax.vjp(partial(jax.nn.gelu, approximate=True), up_rows)
    grad_up = gelu_back(dot_nt(grad_rows, w_down))[0].astype(bf16)
    grad_hidden_two = reduce_product(grad_up, w_up, own_rows)
    by_quarter = lambda grad: grad.reshape(quarters, -1, grad.shape[-1])
    grad_w_down = reduce_weights(by_quarter(dot_tn(activated.astype(bf16), grad_rows)))
    grad_w_up = reduce_weights(by_quarter(dot_tn(grad_up, hidden_two)))
    grad_b_up = token_sum(grad_up)
    unused_two, norm_back_two = jax.vjp(modulate, after_attn, shift_m, scale_m)
    grad_norm_two, grad_shift_m, grad_scale_m = norm_back_two(grad_hidden_two)
    grad_after = grad_y + grad_norm_two

    grad_attn = (gate_a * grad_after).astype(bf16)
    grad_rows = jnp.concatenate(spread(grad_attn))
    grad_gate_a = token_sum(grad_after * attn_out)
    grad_b_out = token_sum(grad_attn)
    grad_attended = dot_nt(grad_rows, w_out).astype(bf16)
    grad_qkv = attend_back(qkv, grad_attended, parts, seen)
    terms = [(grad_qkv[n], w_qkv[n]) for n in range(3)]
    half = grad_qkv.shape[1] // 2
    far = sum(dot_nn(left[half:], right) for left, right in terms)
    near = sum(dot_nn(left[:half], right) for left, right in terms)
    cut = lambda rows: [rows[n : n + own_rows] for n in range(0, half, own_rows)]
    grad_hidden = collect(cut(near) + cut(far))
    grad_w = [by_quarter(dot_tn(grad_qkv[n], hidden)) for n in range(3)]
    grad_w.append(by_quarter(dot_tn(attended, grad_rows)))
    grad_w_attn = reduce_weights(jnp.concatenate(grad_w, axis=1))
    grad_b_qv = jnp.stack([jnp.sum(grad_qkv[n], axis=0, dtype=f32) for n in (0, 2)])
    unused_one, norm_back_one = jax.vjp(modulate, inputs, shift_a, scale_a)
    grad_norm_one, grad_shift_a, grad_scale_a = norm_back_one(grad_hidden)
    grad_inputs = grad_after + grad_norm_one

    grad_mod = (grad_shift_a, grad_scale_a, grad_gate_a, grad_shift_m, grad_scale_m, grad_gate_m)
    small = sum_small(jnp.concatenate(grad_mod, axis=1), grad_b_qv, grad_b_up, grad_b_out, grad_b_down)
    return (grad_inputs, (grad_w_attn, grad_w_up, grad_w_down), small)


def sum_small(grad_mod, grad_b_qv, grad_b_up, grad_b_out, grad_b_down):
    quarters, members = lax.axis_size("tp"), lax.axis_size("ctx")
    own = lax.axis_index("ctx")

    def placed(values):
        count = values.shape[0]
        values = jnp.transpose(values.reshape(count, quarters, 1, -1), (1, 0, 2, 3))
        slots = (jnp.arange(members) == own).astype(f32)[None, None, :, None]
        return (values * slots).reshape(quarters, -1)

    quarter = lambda values: values.reshape(quarters, -1)
    pieces = [
        quarter(grad_mod),
        placed(grad_b_up),
        placed(grad_b_qv),
        quarter(grad_b_out),
        quarter(grad_b_down),
    ]
    sizes = [piece.shape[1] for piece in pieces]
    packed = small_scatter(jnp.concatenate(pieces, axis=1), "tp")
    packed = small_gather(sum_over(packed, "ctx"), "shard")
    edges = [sum(sizes[:n]) for n in range(len(sizes) + 1)]
    parts = [packed[:, edges[n] : edges[n + 1]] for n in range(len(sizes))]
    totals = [jnp.sum(part, axis=0) for part in parts]
    ends = small_gather(jnp.stack(totals[3:]), "tp")
    return (
        parts[0],
        totals[0],
        totals[1],
        totals[2].reshape(2, -1),
        ends[:, 0].reshape(-1),
        ends[:, 1].reshape(-1),
    )


def body(
    video, cond, w_ada, b_ada, w_qkv, b_qv, w_out, b_out, w_up, b_up, w_down, b_down, cotangent
):
    clips, own_frames, own_lines, columns, width = video.shape
    assert clips == 1
    quarters = lax.axis_size("tp")
    own_t = lax.axis_index("ctx")

    cond_act, silu_back = jax.vjp(jax.nn.silu, cond.astype(f32))
    cond_all = small_gather(cond_act.astype(bf16)[0], "shard")
    shard_rows = w_ada.shape[1]
    cond_rows = lax.dynamic_slice_in_dim(
        cond_all, lax.axis_index("shard") * shard_rows, shard_rows, 1
    )
    mod_terms = jnp.einsum("sd,bdm->sbm", cond_rows, w_ada, preferred_element_type=f32)
    mod_part = small_scatter(mod_terms, "shard") + b_ada
    modulation = small_gather(mod_part, "tp")
    modulation = jnp.transpose(modulation, (1, 0, 2)).reshape(2, 6, 1, width)
    mods = [[modulation[b, n] for n in range(6)] for b in range(2)]

    moved = lax.all_to_all(turn(video), "ctx", split_axis=3, concat_axis=2, tiled=True)
    spatial_shape = moved.shape
    temporal_shape = cotangent.shape

    first = fetch_block(0, w_qkv, w_out, w_up, w_down)
    second = fetch_block(1, w_qkv, w_out, w_up, w_down)

    def member_bias(bias, units):
        whole = small_gather(bias, "tp")
        members = whole.reshape(whole.shape[:-1] + (-1, units))
        own = lax.dynamic_index_in_dim(members, own_t, members.ndim - 2, keepdims=False)
        return jnp.moveaxis(own, 0, -2).reshape(bias.shape[:-1] + (-1,)).astype(f32)

    members = lax.axis_size("ctx")
    up_bias = member_bias(b_up, b_up.shape[-1] // members)
    qv_bias = member_bias(b_qv, b_qv.shape[-1] // members)

    rows = lambda values: values.reshape(-1, width)
    spatial = (members, 1)
    frames = temporal_shape[1]
    temporal = (1, GROUP // frames)
    middle, kept_one = forward_block(
        rows(moved).astype(f32), mods[0], first, qv_bias[0], b_out[0], up_bias[0], b_down[0], *spatial
    )
    middle = lax.all_to_all(
        middle.astype(bf16).reshape(spatial_shape), "tp", split_axis=2, concat_axis=1, tiled=True
    )
    result, kept_two = forward_block(
        rows(middle).astype(f32), mods[1], second, qv_bias[1], b_out[1], up_bias[1], b_down[1], *temporal
    )
    grad_moved, weights_two, small_two = backward_block(
        rows(cotangent).astype(f32), kept_two, mods[1], second, *temporal
    )
    grad_middle = lax.all_to_all(
        grad_moved.astype(bf16).reshape(temporal_shape), "tp", split_axis=1, concat_axis=2, tiled=True
    )
    grad_first, weights_one, small_one = backward_block(
        rows(grad_middle).astype(f32), kept_one, mods[0], first, *spatial
    )
    grad_video = lax.all_to_all(
        grad_first.astype(bf16).reshape(spatial_shape), "ctx", split_axis=2, concat_axis=3, tiled=True
    )
    grad_video = turn(grad_video).astype(f32)

    small = (small_one, small_two)
    cond_float = cond_rows.astype(f32)
    grad_w_ada = jnp.stack(
        [
            sum(
                cond_float[s][:, None] * small[b][0][s][None, :]
                for s in range(cond_float.shape[0])
            )
            for b in range(2)
        ]
    )
    grad_cond = sum(
        jnp.dot(small[b][0], w_ada[b].astype(f32).T, precision=highest) for b in range(2)
    )
    grad_cond = small_all_to_all(sum_over(grad_cond, "tp"), "shard").reshape(1, -1)
    grad_cond = silu_back(grad_cond)[0]

    both = (weights_one, weights_two)
    attn = jnp.stack([grads[0] for grads in both])
    up = jnp.stack([grads[1] for grads in both])
    down = jnp.stack([grads[2] for grads in both])
    attn = attn.reshape(2, members, 4, attn.shape[2] // 4, shard_rows)
    grad_w_qkv = jnp.transpose(attn[:, :, :3], (0, 2, 4, 1, 3)).reshape(w_qkv.shape)
    grad_w_out = attn[:, :, 3].reshape(w_out.shape)
    grad_w_up = jnp.transpose(up, (0, 3, 1, 2)).reshape(w_up.shape)
    grad_w_down = down.reshape(w_down.shape)
    stacked = [jnp.stack([small[b][n] for b in range(2)]) for n in range(1, 6)]
    return (
        result.astype(bf16).reshape(temporal_shape),
        grad_video,
        grad_cond,
        grad_w_ada,
        stacked[0],
        grad_w_qkv,
        stacked[2],
        grad_w_out,
        stacked[3],
        grad_w_up,
        stacked[1],
        grad_w_down,
        stacked[4],
    )


def solution(mesh):
    in_specs = (
        P("shard", "ctx", "tp", None, None),
        P("shard", None),
        P(None, "shard", "tp"),
        P(None, "tp"),
        P(None, None, "shard", "tp"),
        P(None, None, "tp"),
        P(None, "tp", "shard"),
        P(),
        P(None, "shard", "tp"),
        P(None, "tp"),
        P(None, "tp", "shard"),
        P(),
        P("shard", None, "tp", "ctx", None),
    )
    out_specs = (
        P("shard", None, "tp", "ctx", None),
        P("shard", "ctx", "tp", None, None),
        P("shard", None),
        P(None, "shard", "tp"),
        P(None, "tp"),
        P(None, None, "shard", "tp"),
        P(None, None, "tp"),
        P(None, "tp", "shard"),
        P(),
        P(None, "shard", "tp"),
        P(None, "tp"),
        P(None, "tp", "shard"),
        P(),
    )
    return jax.shard_map(body, mesh=mesh, in_specs=in_specs, out_specs=out_specs, check_vma=False)
```
